32 devices in a mesh: rep: 2 (over core), width: 4 (over y, x), hid: 4 (over z).
Axes of the slice: x: 2, y: 2, z: 4, core: 2. Of those that a mesh axis runs over, the one named last changes fastest.
Arguments:
- tokens: float32 [128, 5120], P(('rep', 'hid'), 'width'), may hold values from -6 to 6
- cotangent: float32 [128, 5120], P(('rep', 'hid'), 'width'), may hold values from -6 to 6
- w_gate: float32 [5120, 6912], P('width', 'hid'), may hold values from -0.078125 to 0.078125
- w_up: float32 [5120, 6912], P('width', 'hid'), may hold values from -0.078125 to 0.078125
- w_down: float32 [6912, 5120], P('hid', 'width'), may hold values from -0.078125 to 0.078125
Outputs:
- output: float32 [128, 5120], P(('rep', 'hid'), 'width')
- grad_tokens: float32 [128, 5120], P(('rep', 'hid'), 'width')
- grad_gate: float32 [4, 2, 640, 6912], P('width', 'rep', None, 'hid')
- grad_up: float32 [4, 2, 640, 6912], P('width', 'rep', None, 'hid')
- grad_down: float32 [4, 2, 864, 5120], P('hid', 'rep', None, 'width')
The draws below stay inside these ranges and needn't reach their ends.
All inputs are finite; a program needn't handle non-finite values.
Results may differ from the reference program's by a relative error of at most 0.00016.
Values sent between devices are 32-bit elements; how exact they have to be, the bound alone decides.
No kernel may reach another device: no remote copies, remote signals or barrier semaphores. Data moves between devices by JAX's collectives and lax.ppermute only.
A program may use at most 128 MiB of HBM per device.

```python
import jax
import jax.numpy as jnp
from jax import lax

D = 5120
FF = 6912
TOKENS = 128
N_WIDTH = 4
N_HID = 4


def level_of(own_key, shape, shards, smallest, high):
    loudness = 1.0
    for axis_at, parts in shards:
        draws = jax.random.uniform(jax.random.fold_in(jax.random.fold_in(own_key, 6), axis_at), (parts,), jnp.float32, smallest / len(shards), high / len(shards))
        loudness = loudness * jnp.repeat(jnp.exp(draws), shape[axis_at] // parts).reshape((-1,) + (1,) * (len(shape) - 1 - axis_at))
    return loudness


def centred(stream_key, shape, deviation, reach, shards=(), dtype=jnp.bfloat16):
    array = deviation * jax.random.normal(stream_key, shape, jnp.float32)
    if shards:
        array = array * level_of(stream_key, shape, shards, -0.22, 0.18)
    return jnp.clip(array, -reach, reach).astype(dtype)


def setup_inputs(seed: int = 0) -> dict:
    keys = jax.random.split(jax.random.key(seed), 6)
    tokens = centred(keys[0], (TOKENS, D), 1.0, 6.0, ((0, 8), (1, 4)), jnp.float32)
    cotangent = centred(keys[1], (TOKENS, D), 1.0, 6.0, ((0, 8), (1, 4)), jnp.float32)
    w_gate = centred(keys[2], (D, FF), D ** -0.5, 0.078125, ((0, 4), (1, 4)), jnp.float32)
    w_up = centred(keys[3], (D, FF), D ** -0.5, 0.078125, ((0, 4), (1, 4)), jnp.float32)
    w_down = centred(keys[4], (FF, D), FF ** -0.5, 0.078125, ((0, 4), (1, 4)), jnp.float32)
    return {"tokens": tokens, "cotangent": cotangent, "w_gate": w_gate, "w_up": w_up, "w_down": w_down}


def forward_dot(left, right):
    return jnp.dot(left, right, precision=lax.Precision.HIGHEST, preferred_element_type=jnp.float32)


def reference(tokens, cotangent, w_gate, w_up, w_down):
    gate = forward_dot(tokens, w_gate)
    up = forward_dot(tokens, w_up)
    logistic = jax.nn.sigmoid(gate)
    hidden = gate * logistic * up
    output = forward_dot(hidden, w_down)
    grad_hidden = forward_dot(cotangent, w_down.T)
    gate_grad = grad_hidden * up * logistic * (1.0 + gate * (1.0 - logistic))
    up_grad = grad_hidden * gate * logistic
    grad_tokens = forward_dot(gate_grad, w_gate.T) + forward_dot(up_grad, w_up.T)
    grad_gate = forward_dot(tokens.T, gate_grad).reshape(N_WIDTH, 2, D // (2 * N_WIDTH), FF)
    grad_up = forward_dot(tokens.T, up_grad).reshape(N_WIDTH, 2, D // (2 * N_WIDTH), FF)
    grad_down = forward_dot(hidden.T, cotangent).reshape(N_HID, 2, FF // (2 * N_HID), D)
    return output, grad_tokens, grad_gate, grad_up, grad_down
```

```python
import functools

import jax
import jax.numpy as jnp
from jax import lax
from jax.experimental import pallas as pl
from jax.experimental.pallas import tpu as pltpu
from jax.sharding import PartitionSpec as P


BF = jnp.bfloat16
F32 = jnp.float32
MIB = 1 << 20
TILE = 256
VMEM = pl.BlockSpec(memory_space=pltpu.VMEM)
SMEM = pl.BlockSpec(memory_space=pltpu.SMEM)
HBM = pl.BlockSpec(memory_space=pltpu.HBM)
KEPT = pltpu.VMEM
PREPARE_LIMIT = 14


def near(value):
    return pltpu.with_memory_space_constraint(value, pltpu.VMEM)


def split(value):
    high = value.astype(BF)
    low = (value - high.astype(F32)).astype(BF)
    return high, low


def mm(left, right, dims):
    return lax.dot_general(left, right, (dims, ((), ())), preferred_element_type=F32)


def product(both, w_high, w_low, dims):
    rows = both.shape[0] // 2
    wide = mm(both, w_high, dims)
    return wide[:rows] + wide[rows:] + mm(both[:rows], w_low, dims)


def tiles(extent):
    return [(at, min(TILE, extent - at)) for at in range(0, extent, TILE)]


def call(body, out_shape, args, in_specs, scratch, flops, nbytes, limit):
    return pl.pallas_call(
        body,
        out_shape=out_shape,
        in_specs=in_specs,
        out_specs=[VMEM] * len(out_shape),
        scratch_shapes=list(scratch),
        compiler_params=pltpu.CompilerParams(vmem_limit_bytes=limit * MIB),
        cost_estimate=pl.CostEstimate(flops=flops, bytes_accessed=nbytes, transcendentals=0),
    )(*args)


def shape_of(shape, dtype=F32):
    return jax.ShapeDtypeStruct(shape, dtype)


def with_bit(places, mask):
    return [p for p in places if p & mask], [p for p in places if not p & mask]


def prepare_kernel(count, scal, *refs):
    weights, outs = refs[:count], refs[count : 3 * count]
    buffers, sems = refs[3 * count : 4 * count], refs[4 * count]
    hidden = buffers[0].shape[0]
    work = []
    for i in range(count):
        for c, (at, size) in enumerate(tiles(hidden)):
            start = pl.multiple_of(scal[0] * hidden + at, 8)
            copy = pltpu.make_async_copy(
                weights[i].at[pl.ds(start, size), :], buffers[i].at[pl.ds(at, size), :], sems.at[i, c]
            )
            copy.start()
            work.append((copy, i, at, size))
    for copy, i, at, size in work:
        copy.wait()
        high, low = split(buffers[i][at : at + size, :])
        outs[2 * i][at : at + size, :] = high
        outs[2 * i + 1][at : at + size, :] = low


def prepare(scal, weights, hidden):
    depth = weights[0].shape[1]
    count = len(weights)
    return call(
        functools.partial(prepare_kernel, count),
        [KEPT((hidden, depth), BF)] * (2 * count),
        [scal] + [pltpu.with_memory_space_constraint(w, pltpu.HBM) for w in weights],
        [SMEM] + [HBM] * count,
        [pltpu.VMEM((hidden, depth), F32)] * count + [pltpu.SemaphoreType.DMA((count, len(tiles(hidden))))],
        6 * hidden * depth * count,
        8 * hidden * depth * count,
        PREPARE_LIMIT,
    )


def forward_kernel(n, block, count, scal, *refs):
    own, far = refs[:n], refs[n : 2 * n]
    weights = refs[2 * n : 2 * n + 2 * count]
    send, keep, stack, rows_ref, part_ref = refs[2 * n + 2 * count :]
    replica, me = scal[0], scal[1]
    for source, which in ((own, replica), (far, 1 - replica)):
        for s in range(n):
            at = pl.multiple_of((which * n + s) * block, block)
            rows_ref[pl.ds(at, block), :] = source[s][...]
    both = jnp.concatenate(split(rows_ref[...]), axis=0)
    half = stack.shape[1]
    stack[...] = both if half == both.shape[1] else jnp.where(replica == 0, both[:, :half], both[:, half:])
    outs = list(zip((send, keep), with_bit(list(range(n)), 1)))
    for i in range(count):
        part_ref[...] = product(both, weights[2 * i][...], weights[2 * i + 1][...], ((1,), (1,)))
        for ref, chosen in outs:
            for place, label in enumerate(chosen):
                for k in range(2):
                    source = pl.multiple_of((k * n + (label ^ me)) * block, block)
                    at = (2 * place + k) * block
                    ref[i, at : at + block, :] = part_ref[pl.ds(source, block), :]


def forward(scal, own, far, weights, hidden, kept_width):
    n, (block, depth) = len(own), own[0].shape
    rows = 2 * n * block
    count = len(weights) // 2
    return call(
        functools.partial(forward_kernel, n, block, count),
        [shape_of((count, rows // 2, hidden))] * 2 + [shape_of((2 * rows, kept_width), BF)],
        [scal, *own, *far, *weights],
        [SMEM] + [VMEM] * (2 * n + 2 * count),
        [pltpu.VMEM((rows, depth), F32), pltpu.VMEM((rows, hidden), F32)],
        6 * rows * depth * hidden * count,
        4 * count * depth * hidden,
        10,
    )


def load_labels(refs, labels, ref_out, block, n, me, channel):
    for ref, group in zip(refs, labels):
        for place, label in enumerate(group):
            for k in range(2):
                at = pl.multiple_of((k * n + (label ^ me)) * block, block)
                source = (2 * place + k) * block
                ref_out[pl.ds(at, block), :] = ref[channel, source : source + block, :]


def store_owners(part, keep, send, first):
    half = part.shape[0] // 2
    keep[...] = jnp.where(first, part[:half], part[half:])
    send[...] = jnp.where(first, part[half:], part[:half])


def activate_kernel(labels, n, block, scal, *refs):
    parts = refs[: len(labels)]
    w_high, w_low, keep, send, turned, c_gate, c_up, gate_ref, up_ref = refs[len(labels) :]
    replica, me = scal[0], scal[1]
    load_labels(parts, labels, gate_ref, block, n, me, 0)
    load_labels(parts, labels, up_ref, block, n, me, 1)
    gate, up = gate_ref[...], up_ref[...]
    logistic = 1.0 / (1.0 + jnp.exp(-gate))
    swish = gate * logistic
    hid = swish * up
    both = jnp.concatenate(split(hid), axis=0)
    store_owners(product(both, w_high[...], w_low[...], ((1,), (0,))), keep, send, replica == 0)
    c_up[...] = swish
    c_gate[...] = up * logistic * (1.0 + gate * (1.0 - logistic))
    turned[...] = jnp.concatenate(split(hid.T), axis=1)


def backward_kernel(labels, n, block, scal, *refs):
    parts = refs[: len(labels)]
    c_gate, c_up, g_high, g_low, u_high, u_low, keep, send, turned, grad_ref = refs[len(labels) :]
    replica, me = scal[0], scal[1]
    load_labels(parts, labels, grad_ref, block, n, me, 0)
    grad = grad_ref[...]
    gg = grad * c_gate[...]
    ug = grad * c_up[...]
    g_both = jnp.concatenate(split(gg), axis=0)
    u_both = jnp.concatenate(split(ug), axis=0)
    dims = ((1,), (0,))
    part = product(g_both, g_high[...], g_low[...], dims) + product(u_both, u_high[...], u_low[...], dims)
    store_owners(part, keep, send, replica == 0)
    turned[...] = jnp.concatenate([gg.T, ug.T], axis=1)


def outer(left, right):
    rows = right.shape[0] // 2
    high, low = right[:rows], right[rows:]
    return mm(jnp.concatenate([left, left[:, :rows]], 1), jnp.concatenate([high, high, low], 0), ((1,), (0,)))


def down_kernel(left, right, out):
    out[...] = outer(left[...], right[...])


def wide_kernel(scal, own, far, right, g_out, u_out):
    value = jnp.where(pl.program_id(0) == scal[0], own[...], far[...])
    rows = value.shape[1] // 2
    for out, part in ((g_out, value[:, :rows]), (u_out, value[:, rows:])):
        out[...] = outer(jnp.concatenate(split(part), axis=1), right[...])


def add_kernel(group, picks, keep, got, *outs):
    for out, chosen in zip(outs, picks):
        for at, i in enumerate(chosen):
            rows = slice(i * group, (i + 1) * group)
            out[:, at * group : (at + 1) * group, :] = keep[:, rows, :] + got[:, rows, :]


def add_groups(keep, got, group, picks):
    count, _, width = keep.shape
    return call(
        functools.partial(add_kernel, group, picks),
        [shape_of((count, len(chosen) * group, width)) for chosen in picks],
        [keep, got],
        [VMEM] * 2,
        [],
        keep.size,
        12 * keep.size,
        6,
    )


def total_kernel(*refs):
    *parts, out = refs
    value = parts[0][...]
    for part in parts[1:]:
        value = value + part[...]
    out[...] = value


def total_of(parts):
    shape = parts[0].shape
    size = parts[0].size
    return call(
        total_kernel, [shape_of(shape)], parts, [VMEM] * len(parts), [], size * len(parts), 4 * size * len(parts), 4
    )[0]


def shards(n_rep, n_width, n_hid, tokens, cotangent, w_gate, w_up, w_down):
    block, depth = tokens.shape
    full = w_gate.shape[1]
    hidden, half_width = full // n_rep, depth // n_rep
    assert n_rep == 2 and n_width == n_hid
    n = n_hid
    levels = n.bit_length() - 1
    rows = n_rep * n * block
    group = n_rep * block
    replica, place = lax.axis_index("rep"), lax.axis_index("width")
    turned = sum(((place >> i) & 1) << (levels - 1 - i) for i in range(levels))
    me = jnp.where(replica == 0, place, turned)
    scal = jnp.stack([replica, me]).astype(jnp.int32)

    def shift(value, s):
        return lax.ppermute(value, "hid", [(i, i ^ s) for i in range(n)])

    def swap(value):
        return lax.ppermute(value, "rep", [(0, 1), (1, 0)])

    def hop(value, level):
        masks = (1 << level, 1 << (levels - 1 - level))
        pairs = [(r * n + i, r * n + (i ^ masks[r])) for r in range(2) for i in range(n)]
        return lax.ppermute(value, ("rep", "width"), pairs)

    def gather(value):
        own = [value] + [shift(value, s) for s in range(1, n)]
        return own, [swap(v) for v in own]

    def reduce_over_width(send, keep):
        labels = list(range(n))
        for level in range(levels):
            labels = with_bit(labels, 1 << level)[1]
            got = hop(send, level)
            if level + 1 < levels:
                picks = [[labels.index(p) for p in some] for some in with_bit(labels, 2 << level)]
                send, keep = add_groups(keep, got, group, picks)
        held = [([0], add_groups(keep, got, group, [[0]])[0])]
        for level in reversed(range(levels)):
            held = held + [([p ^ (1 << level) for p in some], hop(value, level)) for some, value in held]
        return [value for _, value in held], [some for some, _ in held]

    def to_owner(keep, send):
        got = swap(send)
        blocks = add_groups(keep[None], got[None], block, [[s] for s in range(n)])
        blocks = [b[0] for b in blocks]
        return total_of([blocks[0]] + [shift(blocks[s], s) for s in range(1, n)])

    x_own, x_far = gather(tokens)
    y_own, y_far = gather(cotangent)
    wgu = prepare(scal, [w_gate.T, w_up.T], hidden)
    wd = prepare(scal, [w_down], hidden)
    wgu, wd = [near(w) for w in wgu], [near(w) for w in wd]
    *outs, x_half = forward(scal, x_own, x_far, wgu, hidden, half_width)
    gu_parts, labels = reduce_over_width(*outs)
    *outs, y_both = forward(scal, y_own, y_far, wd, hidden, depth)
    gh_parts, _ = reduce_over_width(*outs)

    narrow = [shape_of((n * block, depth))] * 2
    keep, send, hid_turned, c_gate, c_up = call(
        functools.partial(activate_kernel, labels, n, block),
        narrow + [shape_of((hidden, 2 * rows), BF)] + [shape_of((rows, hidden))] * 2,
        [scal, *gu_parts, *wd],
        [SMEM] + [VMEM] * (len(gu_parts) + 2),
        [pltpu.VMEM((rows, hidden), F32)] * 2,
        6 * rows * hidden * depth,
        4 * hidden * depth,
        8,
    )
    output = to_owner(keep, send)

    tile = depth // 2 if depth % TILE == 0 else depth
    grad_down = pl.pallas_call(
        down_kernel,
        out_shape=shape_of((hidden, depth)),
        in_specs=[
            pl.BlockSpec((hidden, 2 * rows), lambda i: (0, 0)),
            pl.BlockSpec((2 * rows, tile), lambda i: (0, i)),
        ],
        out_specs=pl.BlockSpec((hidden, tile), lambda i: (0, i)),
        grid=(depth // tile,),
        compiler_params=pltpu.CompilerParams(vmem_limit_bytes=14 * MIB),
        cost_estimate=pl.CostEstimate(flops=6 * rows * hidden * depth, bytes_accessed=4 * hidden * depth, transcendentals=0),
        name="down",
    )(hid_turned, y_both)

    keep, send, grads = call(
        functools.partial(backward_kernel, labels, n, block),
        narrow + [shape_of((hidden, 2 * rows))],
        [scal, *gh_parts, c_gate, c_up, *wgu],
        [SMEM] + [VMEM] * (len(gh_parts) + 6),
        [pltpu.VMEM((rows, hidden), F32)],
        12 * rows * hidden * depth,
        8 * hidden * depth,
        8,
    )
    far = swap(grads)
    grad_tokens = to_owner(keep, send)

    chunks = 2 if hidden % 16 == 0 else 1
    lines = hidden // chunks
    side = pl.BlockSpec((lines, 2 * rows), lambda i, j: (j, 0))
    grad_gate, grad_up = pl.pallas_call(
        wide_kernel,
        out_shape=[shape_of((full, half_width))] * 2,
        in_specs=[SMEM, side, side, pl.BlockSpec((2 * rows, half_width), lambda i, j: (0, 0))],
        out_specs=[pl.BlockSpec((lines, half_width), lambda i, j: (i * chunks + j, 0))] * 2,
        grid=(n_rep, chunks),
        compiler_params=pltpu.CompilerParams(vmem_limit_bytes=14 * MIB),
        cost_estimate=pl.CostEstimate(
            flops=12 * rows * half_width * full, bytes_accessed=8 * half_width * full, transcendentals=0
        ),
        name="wide",
    )(scal, grads, far, x_half)
    return (
        output,
        grad_tokens,
        grad_gate.T.reshape(1, 1, half_width, full),
        grad_up.T.reshape(1, 1, half_width, full),
        grad_down.reshape(1, 1, hidden, depth),
    )


def solution(mesh):
    sizes = [mesh.shape[a] for a in ("rep", "width", "hid")]
    return jax.shard_map(
        functools.partial(shards, *sizes),
        mesh=mesh,
        in_specs=(
            P(("rep", "hid"), "width"),
            P(("rep", "hid"), "width"),
            P("width", "hid"),
            P("width", "hid"),
            P("hid", "width"),
        ),
        out_specs=(
            P(("rep", "hid"), "width"),
            P(("rep", "hid"), "width"),
            P("width", "rep", None, "hid"),
            P("width", "rep", None, "hid"),
            P("hid", "rep", None, "width"),
        ),
        check_vma=False,
    )
```

```python
import functools

import jax
import jax.numpy as jnp
from jax import lax
from jax.experimental import pallas as pl
from jax.experimental.pallas import tpu as pltpu
from jax.sharding import PartitionSpec as P


BF = jnp.bfloat16
F32 = jnp.float32
MIB = 1 << 20
TILE = 256
VMEM = pl.BlockSpec(memory_space=pltpu.VMEM)
SMEM = pl.BlockSpec(memory_space=pltpu.SMEM)
HBM = pl.BlockSpec(memory_space=pltpu.HBM)
KEPT = pltpu.VMEM
PREPARE_LIMIT = 20


def near(value):
    return pltpu.with_memory_space_constraint(value, pltpu.VMEM)


def split(value):
    high = value.astype(BF)
    low = (value - high.astype(F32)).astype(BF)
    return high, low


def mm(left, right, dims):
    return lax.dot_general(left, right, (dims, ((), ())), preferred_element_type=F32)


def product(both, w_high, w_low, dims):
    rows = both.shape[0] // 2
    wide = mm(both, w_high, dims)
    return wide[:rows] + wide[rows:] + mm(both[:rows], w_low, dims)


def tiles(extent):
    return [(at, min(TILE, extent - at)) for at in range(0, extent, TILE)]


def call(body, out_shape, args, in_specs, scratch, flops, nbytes, limit, out_spec=VMEM):
    return pl.pallas_call(
        body,
        out_shape=out_shape,
        in_specs=in_specs,
        out_specs=[out_spec] * len(out_shape),
        scratch_shapes=list(scratch),
        compiler_params=pltpu.CompilerParams(vmem_limit_bytes=limit * MIB),
        cost_estimate=pl.CostEstimate(flops=flops, bytes_accessed=nbytes, transcendentals=0),
    )(*args)


def shape_of(shape, dtype=F32):
    return jax.ShapeDtypeStruct(shape, dtype)


def with_bit(places, mask):
    return [p for p in places if p & mask], [p for p in places if not p & mask]


def prepare_kernel(count, scal, *refs):
    weights, outs = refs[:count], refs[count : 3 * count]
    buffers, sems = refs[3 * count : 4 * count], refs[4 * count]
    hidden = buffers[0].shape[0]
    work = []
    for i in range(count):
        for c, (at, size) in enumerate(tiles(hidden)):
            start = pl.multiple_of(scal[0] * hidden + at, 8)
            copy = pltpu.make_async_copy(
                weights[i].at[pl.ds(start, size), :], buffers[i].at[pl.ds(at, size), :], sems.at[i, c]
            )
            copy.start()
            work.append((copy, i, at, size))
    for copy, i, at, size in work:
        copy.wait()
        high, low = split(buffers[i][at : at + size, :])
        outs[2 * i][at : at + size, :] = high
        outs[2 * i + 1][at : at + size, :] = low


def prepare(scal, weights, hidden):
    depth = weights[0].shape[1]
    count = len(weights)
    return call(
        functools.partial(prepare_kernel, count),
        [KEPT((hidden, depth), BF)] * (2 * count),
        [scal] + [pltpu.with_memory_space_constraint(w, pltpu.HBM) for w in weights],
        [SMEM] + [HBM] * count,
        [pltpu.VMEM((hidden, depth), F32)] * count + [pltpu.SemaphoreType.DMA((count, len(tiles(hidden))))],
        6 * hidden * depth * count,
        8 * hidden * depth * count,
        PREPARE_LIMIT,
    )


def forward_kernel(n, block, count, scal, *refs):
    own, far = refs[:n], refs[n : 2 * n]
    weights = refs[2 * n : 2 * n + 2 * count]
    send, keep, stack, rows_ref, part_ref = refs[2 * n + 2 * count :]
    replica, me = scal[0], scal[1]
    for source, which in ((own, replica), (far, 1 - replica)):
        for s in range(n):
            at = pl.multiple_of((which * n + s) * block, block)
            rows_ref[pl.ds(at, block), :] = source[s][...]
    both = jnp.concatenate(split(rows_ref[...]), axis=0)
    half = stack.shape[1]
    stack[...] = both if half == both.shape[1] else jnp.where(replica == 0, both[:, :half], both[:, half:])
    outs = list(zip((send, keep), with_bit(list(range(n)), 1)))
    for i in range(count):
        part_ref[...] = product(both, weights[2 * i][...], weights[2 * i + 1][...], ((1,), (1,)))
        for ref, chosen in outs:
            for place, label in enumerate(chosen):
                for k in range(2):
                    source = pl.multiple_of((k * n + (label ^ me)) * block, block)
                    at = (2 * place + k) * block
                    ref[i, at : at + block, :] = part_ref[pl.ds(source, block), :]


def forward(scal, own, far, weights, hidden, kept_width):
    n, (block, depth) = len(own), own[0].shape
    rows = 2 * n * block
    count = len(weights) // 2
    return call(
        functools.partial(forward_kernel, n, block, count),
        [shape_of((count, rows // 2, hidden))] * 2 + [shape_of((2 * rows, kept_width), BF)],
        [scal, *own, *far, *weights],
        [SMEM] + [VMEM] * (2 * n + 2 * count),
        [pltpu.VMEM((rows, depth), F32), pltpu.VMEM((rows, hidden), F32)],
        6 * rows * depth * hidden * count,
        4 * count * depth * hidden,
        10,
    )


def load_labels(refs, labels, ref_out, block, n, me, channel):
    for ref, group in zip(refs, labels):
        for place, label in enumerate(group):
            for k in range(2):
                at = pl.multiple_of((k * n + (label ^ me)) * block, block)
                source = (2 * place + k) * block
                ref_out[pl.ds(at, block), :] = ref[channel, source : source + block, :]


def store_owners(part, keep, send, first):
    half = part.shape[0] // 2
    keep[...] = jnp.where(first, part[:half], part[half:])
    send[...] = jnp.where(first, part[half:], part[:half])


def activate_kernel(labels, n, block, scal, *refs):
    parts = refs[: len(labels)]
    w_high, w_low, keep, send, turned, c_gate, c_up, gate_ref, up_ref = refs[len(labels) :]
    replica, me = scal[0], scal[1]
    load_labels(parts, labels, gate_ref, block, n, me, 0)
    load_labels(parts, labels, up_ref, block, n, me, 1)
    gate, up = gate_ref[...], up_ref[...]
    logistic = 1.0 / (1.0 + jnp.exp(-gate))
    swish = gate * logistic
    hid = swish * up
    both = jnp.concatenate(split(hid), axis=0)
    store_owners(product(both, w_high[...], w_low[...], ((1,), (0,))), keep, send, replica == 0)
    c_up[...] = swish
    c_gate[...] = up * logistic * (1.0 + gate * (1.0 - logistic))
    turned[...] = jnp.concatenate(split(hid.T), axis=1)


def backward_kernel(labels, n, block, scal, *refs):
    parts = refs[: len(labels)]
    c_gate, c_up, g_high, g_low, u_high, u_low, keep, send, turned, grad_ref = refs[len(labels) :]
    replica, me = scal[0], scal[1]
    load_labels(parts, labels, grad_ref, block, n, me, 0)
    grad = grad_ref[...]
    gg = grad * c_gate[...]
    ug = grad * c_up[...]
    g_both = jnp.concatenate(split(gg), axis=0)
    u_both = jnp.concatenate(split(ug), axis=0)
    dims = ((1,), (0,))
    part = product(g_both, g_high[...], g_low[...], dims) + product(u_both, u_high[...], u_low[...], dims)
    store_owners(part, keep, send, replica == 0)
    turned[...] = jnp.concatenate([gg.T, ug.T], axis=1)


def outer(left, right):
    rows = right.shape[0] // 2
    high, low = right[:rows], right[rows:]
    return mm(jnp.concatenate([left, left[:, :rows]], 1), jnp.concatenate([high, high, low], 0), ((1,), (0,)))


def pieces(extent):
    cuts = [extent * i // 4 // 16 * 16 for i in range(4)] + [extent]
    return [(at, end - at) for at, end in zip(cuts, cuts[1:])]


def weights_kernel(scal, own, far, x_right, h_left, y_right, g_out, u_out, d_out, g_buffer, u_buffer, d_buffer, sems):
    lines, rows = own.shape[0], own.shape[1] // 2
    copies = []

    def send(buffer, out, start, size):
        rows_at = pl.ds(pl.multiple_of(start, 8), size)
        copy = pltpu.make_async_copy(buffer, out.at[rows_at, :], sems.at[len(copies)])
        copy.start()
        copies.append(copy)

    for at, size in pieces(lines):
        piece = d_buffer.at[pl.ds(at, size), :]
        d_buffer[at : at + size, :] = outer(h_left[at : at + size, :], y_right[...])
        send(piece, d_out, at, size)
    for out, buffer, first in ((g_out, g_buffer, 0), (u_out, u_buffer, rows)):
        for k, (source, which) in enumerate(((own, scal[0]), (far, 1 - scal[0]))):
            for at, size in pieces(lines):
                left = jnp.concatenate(split(source[at : at + size, first : first + rows]), axis=1)
                here = k * lines + at
                buffer[here : here + size, :] = outer(left, x_right[...])
                send(buffer.at[pl.ds(here, size), :], out, which * lines + at, size)
    for copy in copies:
        copy.wait()


def add_kernel(group, picks, keep, got, *outs):
    for out, chosen in zip(outs, picks):
        for at, i in enumerate(chosen):
            rows = slice(i * group, (i + 1) * group)
            out[:, at * group : (at + 1) * group, :] = keep[:, rows, :] + got[:, rows, :]


def add_groups(keep, got, group, picks):
    count, _, width = keep.shape
    return call(
        functools.partial(add_kernel, group, picks),
        [shape_of((count, len(chosen) * group, width)) for chosen in picks],
        [keep, got],
        [VMEM] * 2,
        [],
        keep.size,
        12 * keep.size,
        6,
    )


def finish_kernel(counts, *refs):
    parts, outs = refs[: sum(counts)], refs[sum(counts) :]
    for out, count in zip(outs, counts):
        value = parts[0][...]
        for part in parts[1:count]:
            value = value + part[...]
        out[...] = value
        parts = parts[count:]


def finish(groups):
    shape, size = groups[0][0].shape, groups[0][0].size
    parts = [part for group in groups for part in group]
    return call(
        functools.partial(finish_kernel, [len(group) for group in groups]),
        [shape_of(shape)] * len(groups),
        parts,
        [VMEM] * len(parts),
        [],
        size * len(parts),
        4 * size * len(parts),
        4,
    )


def shards(n_rep, n_width, n_hid, tokens, cotangent, w_gate, w_up, w_down):
    block, depth = tokens.shape
    full = w_gate.shape[1]
    hidden, half_width = full // n_rep, depth // n_rep
    assert n_rep == 2 and n_width == n_hid
    n = n_hid
    levels = n.bit_length() - 1
    rows = n_rep * n * block
    group = n_rep * block
    replica, place = lax.axis_index("rep"), lax.axis_index("width")
    turned = sum(((place >> i) & 1) << (levels - 1 - i) for i in range(levels))
    me = jnp.where(replica == 0, place, turned)
    scal = jnp.stack([replica, me]).astype(jnp.int32)

    def shift(value, s):
        return lax.ppermute(value, "hid", [(i, i ^ s) for i in range(n)])

    def swap(value):
        return lax.ppermute(value, "rep", [(0, 1), (1, 0)])

    def hop(value, level):
        masks = (1 << level, 1 << (levels - 1 - level))
        pairs = [(r * n + i, r * n + (i ^ masks[r])) for r in range(2) for i in range(n)]
        return lax.ppermute(value, ("rep", "width"), pairs)

    def gather(value):
        own = [value] + [shift(value, s) for s in reversed(range(1, n))][::-1]
        return own, [swap(v) for v in own]

    def reduce_over_width(send, keep):
        labels = list(range(n))
        for level in range(levels):
            labels = with_bit(labels, 1 << level)[1]
            got = hop(send, level)
            if level + 1 < levels:
                picks = [[labels.index(p) for p in some] for some in with_bit(labels, 2 << level)]
                send, keep = add_groups(keep, got, group, picks)
        held = [([0], add_groups(keep, got, group, [[0]])[0])]
        for level in reversed(range(levels)):
            held = held + [([p ^ (1 << level) for p in some], hop(value, level)) for some, value in held]
        return [value for _, value in held], [some for some, _ in held]

    def to_owner(keep, send):
        got = swap(send)
        blocks = add_groups(keep[None], got[None], block, [[s] for s in range(n)])
        moved = [shift(blocks[s][0], s) for s in reversed(range(1, n))]
        return [blocks[0][0]] + moved

    def to_owner_by_hops(keep, send):
        got = swap(send)
        keep, got = keep[None], got[None]
        labels = list(range(n))
        for level in range(levels):
            picks = [[labels.index(p) for p in some] for some in with_bit(labels, 1 << level)]
            labels = with_bit(labels, 1 << level)[1]
            send, keep = add_groups(keep, got, block, picks)
            got = shift(send, 1 << level)
        return [keep[0], got[0]]

    x_own, x_far = gather(tokens)
    y_own, y_far = gather(cotangent)
    prepared = [near(w) for w in prepare(scal, [w_gate.T, w_up.T, w_down], hidden)]
    wgu, wd = prepared[:4], prepared[4:]
    *outs, x_half = forward(scal, x_own, x_far, wgu, hidden, half_width)
    gu_parts, labels = reduce_over_width(*outs)
    *outs, y_both = forward(scal, y_own, y_far, wd, hidden, depth)
    gh_parts, _ = reduce_over_width(*outs)

    narrow = [shape_of((n * block, depth))] * 2
    keep, send, hid_turned, c_gate, c_up = call(
        functools.partial(activate_kernel, labels, n, block),
        narrow + [shape_of((hidden, 2 * rows), BF)] + [shape_of((rows, hidden))] * 2,
        [scal, *gu_parts, *wd],
        [SMEM] + [VMEM] * (len(gu_parts) + 2),
        [pltpu.VMEM((rows, hidden), F32)] * 2,
        6 * rows * hidden * depth,
        4 * hidden * depth,
        8,
    )
    output_parts = to_owner_by_hops(keep, send)

    keep, send, grads = call(
        functools.partial(backward_kernel, labels, n, block),
        narrow + [shape_of((hidden, 2 * rows))],
        [scal, *gh_parts, c_gate, c_up, *wgu],
        [SMEM] + [VMEM] * (len(gh_parts) + 6),
        [pltpu.VMEM((rows, hidden), F32)],
        12 * rows * hidden * depth,
        8 * hidden * depth,
        8,
    )
    far = swap(grads)
    token_parts = to_owner(keep, send)

    shapes = [(full, half_width), (full, half_width), (hidden, depth)]
    grad_gate, grad_up, grad_down = call(
        weights_kernel,
        [shape_of(shape) for shape in shapes],
        [scal, grads, far, x_half, hid_turned, y_both],
        [SMEM] + [VMEM] * 5,
        [pltpu.VMEM(shape, F32) for shape in shapes] + [pltpu.SemaphoreType.DMA((20,))],
        18 * rows * half_width * full,
        12 * half_width * full,
        20,
        HBM,
    )
    output, grad_tokens = finish([output_parts, token_parts])
    return (
        output,
        grad_tokens,
        grad_gate.T.reshape(1, 1, half_width, full),
        grad_up.T.reshape(1, 1, half_width, full),
        grad_down.reshape(1, 1, hidden, depth),
    )


def solution(mesh):
    sizes = [mesh.shape[a] for a in ("rep", "width", "hid")]
    return jax.shard_map(
        functools.partial(shards, *sizes),
        mesh=mesh,
        in_specs=(
            P(("rep", "hid"), "width"),
            P(("rep", "hid"), "width"),
            P("width", "hid"),
            P("width", "hid"),
            P("hid", "width"),
        ),
        out_specs=(
            P(("rep", "hid"), "width"),
            P(("rep", "hid"), "width"),
            P("width", "rep", None, "hid"),
            P("width", "rep", None, "hid"),
            P("hid", "rep", None, "width"),
        ),
        check_vma=False,
    )
```

```python
import functools

import jax
import jax.numpy as jnp
from jax import lax
from jax.experimental import pallas as pl
from jax.experimental.pallas import tpu as pltpu
from jax.sharding import PartitionSpec as P


BF = jnp.bfloat16
F32 = jnp.float32
MIB = 1 << 20
TILE = 256
VMEM = pl.BlockSpec(memory_space=pltpu.VMEM)
SMEM = pl.BlockSpec(memory_space=pltpu.SMEM)
HBM = pl.BlockSpec(memory_space=pltpu.HBM)
KEPT = pltpu.VMEM
PREPARE_LIMIT = 20


def near(value):
    return pltpu.with_memory_space_constraint(value, pltpu.VMEM)


def split(value):
    high = value.astype(BF)
    low = (value - high.astype(F32)).astype(BF)
    return high, low


def mm(left, right, dims):
    return lax.dot_general(left, right, (dims, ((), ())), preferred_element_type=F32)


def product(both, w_high, w_low, dims):
    rows = both.shape[0] // 2
    wide = mm(both, w_high, dims)
    return wide[:rows] + wide[rows:] + mm(both[:rows], w_low, dims)


def turned_product(both, w_high, w_low):
    rows = both.shape[0] // 2
    dims = ((1,), (1,))
    wide = mm(w_high, both, dims)
    return (wide[:, :rows] + wide[:, rows:] + mm(w_low, both[:rows], dims)).T


def tiles(extent):
    return [(at, min(TILE, extent - at)) for at in range(0, extent, TILE)]


def call(body, out_shape, args, in_specs, scratch, flops, nbytes, limit, out_spec=VMEM):
    return pl.pallas_call(
        body,
        out_shape=out_shape,
        in_specs=in_specs,
        out_specs=[out_spec] * len(out_shape),
        scratch_shapes=list(scratch),
        compiler_params=pltpu.CompilerParams(vmem_limit_bytes=limit * MIB),
        cost_estimate=pl.CostEstimate(flops=flops, bytes_accessed=nbytes, transcendentals=0),
    )(*args)


def shape_of(shape, dtype=F32):
    return jax.ShapeDtypeStruct(shape, dtype)


def with_bit(places, mask):
    return [p for p in places if p & mask], [p for p in places if not p & mask]


def prepare_kernel(count, scal, *refs):
    weights, outs = refs[:count], refs[count : 3 * count]
    buffers, sems = refs[3 * count : 4 * count], refs[4 * count]
    hidden = buffers[0].shape[0]
    work = []
    for i in range(count):
        for c, (at, size) in enumerate(tiles(hidden)):
            start = pl.multiple_of(scal[0] * hidden + at, 8)
            copy = pltpu.make_async_copy(
                weights[i].at[pl.ds(start, size), :], buffers[i].at[pl.ds(at, size), :], sems.at[i, c]
            )
            copy.start()
            work.append((copy, i, at, size))
    for copy, i, at, size in work:
        copy.wait()
        high, low = split(buffers[i][at : at + size, :])
        outs[2 * i][at : at + size, :] = high
        outs[2 * i + 1][at : at + size, :] = low


def prepare(scal, weights, hidden):
    depth = weights[0].shape[1]
    count = len(weights)
    return call(
        functools.partial(prepare_kernel, count),
        [KEPT((hidden, depth), BF)] * (2 * count),
        [scal] + [pltpu.with_memory_space_constraint(w, pltpu.HBM) for w in weights],
        [SMEM] + [HBM] * count,
        [pltpu.VMEM((hidden, depth), F32)] * count + [pltpu.SemaphoreType.DMA((count, len(tiles(hidden))))],
        6 * hidden * depth * count,
        8 * hidden * depth * count,
        PREPARE_LIMIT,
    )


def forward_kernel(n, block, count, scal, *refs):
    own, far = refs[:n], refs[n : 2 * n]
    weights = refs[2 * n : 2 * n + 2 * count]
    send, keep, stack, rows_ref, part_ref = refs[2 * n + 2 * count :]
    replica, me = scal[0], scal[1]
    for source, which in ((own, replica), (far, 1 - replica)):
        for s in range(n):
            at = pl.multiple_of((which * n + s) * block, block)
            rows_ref[pl.ds(at, block), :] = source[s][...]
    both = jnp.concatenate(split(rows_ref[...]), axis=0)
    half = stack.shape[1]
    stack[...] = both if half == both.shape[1] else jnp.where(replica == 0, both[:, :half], both[:, half:])
    outs = list(zip((send, keep), with_bit(list(range(n)), 1)))
    for i in range(count):
        part_ref[...] = turned_product(both, weights[2 * i][...], weights[2 * i + 1][...])
        for ref, chosen in outs:
            for place, label in enumerate(chosen):
                for k in range(2):
                    source = pl.multiple_of((k * n + (label ^ me)) * block, block)
                    at = (2 * place + k) * block
                    ref[i, at : at + block, :] = part_ref[pl.ds(source, block), :]


def forward(scal, own, far, weights, hidden, kept_width):
    n, (block, depth) = len(own), own[0].shape
    rows = 2 * n * block
    count = len(weights) // 2
    return call(
        functools.partial(forward_kernel, n, block, count),
        [shape_of((count, rows // 2, hidden))] * 2 + [shape_of((2 * rows, kept_width), BF)],
        [scal, *own, *far, *weights],
        [SMEM] + [VMEM] * (2 * n + 2 * count),
        [pltpu.VMEM((rows, depth), F32), pltpu.VMEM((rows, hidden), F32)],
        6 * rows * depth * hidden * count,
        4 * count * depth * hidden,
        10,
    )


def load_labels(refs, labels, ref_out, block, n, me, channel):
    for ref, group in zip(refs, labels):
        for place, label in enumerate(group):
            for k in range(2):
                at = pl.multiple_of((k * n + (label ^ me)) * block, block)
                source = (2 * place + k) * block
                ref_out[pl.ds(at, block), :] = ref[channel, source : source + block, :]


def store_owners(part, keep, send, first):
    half = part.shape[0] // 2
    keep[...] = jnp.where(first, part[:half], part[half:])
    send[...] = jnp.where(first, part[half:], part[:half])


def activate_kernel(labels, n, block, scal, *refs):
    parts = refs[: len(labels)]
    w_high, w_low, keep, send, turned, c_gate, c_up, gate_ref, up_ref = refs[len(labels) :]
    replica, me = scal[0], scal[1]
    load_labels(parts, labels, gate_ref, block, n, me, 0)
    load_labels(parts, labels, up_ref, block, n, me, 1)
    gate, up = gate_ref[...], up_ref[...]
    logistic = 1.0 / (1.0 + jnp.exp(-gate))
    swish = gate * logistic
    hid = swish * up
    both = jnp.concatenate(split(hid), axis=0)
    store_owners(product(both, w_high[...], w_low[...], ((1,), (0,))), keep, send, replica == 0)
    c_up[...] = swish
    c_gate[...] = up * logistic * (1.0 + gate * (1.0 - logistic))
    turned[...] = jnp.concatenate(split(hid.T), axis=1)


def backward_kernel(labels, n, block, scal, *refs):
    parts = refs[: len(labels)]
    c_gate, c_up, g_high, g_low, u_high, u_low, keep, send, turned, grad_ref = refs[len(labels) :]
    replica, me = scal[0], scal[1]
    load_labels(parts, labels, grad_ref, block, n, me, 0)
    grad = grad_ref[...]
    gg = grad * c_gate[...]
    ug = grad * c_up[...]
    g_both = jnp.concatenate(split(gg), axis=0)
    u_both = jnp.concatenate(split(ug), axis=0)
    dims = ((1,), (0,))
    part = product(g_both, g_high[...], g_low[...], dims) + product(u_both, u_high[...], u_low[...], dims)
    store_owners(part, keep, send, replica == 0)
    turned[...] = jnp.concatenate([gg.T, ug.T], axis=1)


def outer(left, right):
    rows = right.shape[0] // 2
    high, low = right[:rows], right[rows:]
    return mm(jnp.concatenate([left, left[:, :rows]], 1), jnp.concatenate([high, high, low], 0), ((1,), (0,)))


def pieces(extent):
    cuts = [extent * i // 4 // 16 * 16 for i in range(4)] + [extent]
    return [(at, end - at) for at, end in zip(cuts, cuts[1:])]


def writer(sems):
    copies = []

    def send(buffer, out, start, size):
        rows = pl.ds(pl.multiple_of(start, 8), size)
        copy = pltpu.make_async_copy(buffer, out.at[rows, :], sems.at[len(copies)])
        copy.start()
        copies.append(copy)

    return copies, send


def down_kernel(left, right, out, buffer, sems):
    copies, send = writer(sems)
    for at, size in pieces(left.shape[0]):
        buffer[at : at + size, :] = outer(left[at : at + size, :], right[...])
        send(buffer.at[pl.ds(at, size), :], out, at, size)
    for copy in copies:
        copy.wait()


def weights_kernel(scal, own, far, right, g_out, u_out, g_buffer, u_buffer, sems):
    lines, rows = own.shape[0], own.shape[1] // 2
    copies, send = writer(sems)
    for out, buffer, first in ((g_out, g_buffer, 0), (u_out, u_buffer, rows)):
        for k, (source, which) in enumerate(((own, scal[0]), (far, 1 - scal[0]))):
            for at, size in pieces(lines):
                left = jnp.concatenate(split(source[at : at + size, first : first + rows]), axis=1)
                here = k * lines + at
                buffer[here : here + size, :] = outer(left, right[...])
                send(buffer.at[pl.ds(here, size), :], out, which * lines + at, size)
    for copy in copies:
        copy.wait()


def add_kernel(group, picks, keep, got, *outs):
    for out, chosen in zip(outs, picks):
        for at, i in enumerate(chosen):
            rows = slice(i * group, (i + 1) * group)
            out[:, at * group : (at + 1) * group, :] = keep[:, rows, :] + got[:, rows, :]


def add_groups(keep, got, group, picks):
    count, _, width = keep.shape
    return call(
        functools.partial(add_kernel, group, picks),
        [shape_of((count, len(chosen) * group, width)) for chosen in picks],
        [keep, got],
        [VMEM] * 2,
        [],
        keep.size,
        12 * keep.size,
        6,
    )


def finish_kernel(counts, *refs):
    parts, outs = refs[: sum(counts)], refs[sum(counts) :]
    for out, count in zip(outs, counts):
        value = parts[0][...]
        for part in parts[1:count]:
            value = value + part[...]
        out[...] = value
        parts = parts[count:]


def finish(groups):
    shape, size = groups[0][0].shape, groups[0][0].size
    parts = [part for group in groups for part in group]
    return call(
        functools.partial(finish_kernel, [len(group) for group in groups]),
        [shape_of(shape)] * len(groups),
        parts,
        [VMEM] * len(parts),
        [],
        size * len(parts),
        4 * size * len(parts),
        4,
    )


def shards(n_rep, n_width, n_hid, tokens, cotangent, w_gate, w_up, w_down):
    block, depth = tokens.shape
    full = w_gate.shape[1]
    hidden, half_width = full // n_rep, depth // n_rep
    assert n_rep == 2 and n_width == n_hid
    n = n_hid
    levels = n.bit_length() - 1
    rows = n_rep * n * block
    group = n_rep * block
    replica, place = lax.axis_index("rep"), lax.axis_index("width")
    turned = sum(((place >> i) & 1) << (levels - 1 - i) for i in range(levels))
    me = jnp.where(replica == 0, place, turned)
    scal = jnp.stack([replica, me]).astype(jnp.int32)

    def shift(value, s):
        return lax.ppermute(value, "hid", [(i, i ^ s) for i in range(n)])

    def swap(value):
        return lax.ppermute(value, "rep", [(0, 1), (1, 0)])

    def hop(value, level):
        masks = (1 << level, 1 << (levels - 1 - level))
        pairs = [(r * n + i, r * n + (i ^ masks[r])) for r in range(2) for i in range(n)]
        return lax.ppermute(value, ("rep", "width"), pairs)

    def gather(value):
        own = [value] + [shift(value, s) for s in reversed(range(1, n))][::-1]
        return own, [swap(v) for v in own]

    def reduce_over_width(send, keep):
        labels = list(range(n))
        for level in range(levels):
            labels = with_bit(labels, 1 << level)[1]
            got = hop(send, level)
            if level + 1 < levels:
                picks = [[labels.index(p) for p in some] for some in with_bit(labels, 2 << level)]
                send, keep = add_groups(keep, got, group, picks)
        held = [([0], add_groups(keep, got, group, [[0]])[0])]
        for level in reversed(range(levels)):
            held = held + [
                ([p ^ (1 << level) for p in some], hop(value, level))
                for some, value in held
            ]
        return [value for _, value in held], [some for some, _ in held]

    def to_owner(keep, send):
        got = swap(send)
        blocks = add_groups(keep[None], got[None], block, [[s] for s in range(n)])
        moved = [shift(blocks[s][0], s) for s in reversed(range(1, n))]
        return [blocks[0][0]] + moved

    def to_owner_by_hops(keep, send):
        got = swap(send)
        keep, got = keep[None], got[None]
        labels = list(range(n))
        for level in range(levels):
            picks = [[labels.index(p) for p in some] for some in with_bit(labels, 1 << level)]
            labels = with_bit(labels, 1 << level)[1]
            send, keep = add_groups(keep, got, block, picks)
            got = shift(send, 1 << level)
        return [keep[0], got[0]]

    x_own, x_far = gather(tokens)
    y_own, y_far = gather(cotangent)
    prepared = [near(w) for w in prepare(scal, [w_gate.T, w_up.T, w_down], hidden)]
    wgu, wd = prepared[:4], prepared[4:]
    *outs, x_half = forward(scal, x_own, x_far, wgu, hidden, half_width)
    gu_parts, labels = reduce_over_width(*outs)
    *outs, y_both = forward(scal, y_own, y_far, wd, hidden, depth)
    gh_parts, _ = reduce_over_width(*outs)

    narrow = [shape_of((n * block, depth))] * 2
    keep, send, hid_turned, c_gate, c_up = call(
        functools.partial(activate_kernel, labels, n, block),
        narrow + [shape_of((hidden, 2 * rows), BF)] + [shape_of((rows, hidden))] * 2,
        [scal, *gu_parts, *wd],
        [SMEM] + [VMEM] * (len(gu_parts) + 2),
        [pltpu.VMEM((rows, hidden), F32)] * 2,
        6 * rows * hidden * depth,
        4 * hidden * depth,
        8,
    )
    output_parts = to_owner_by_hops(keep, send)

    keep, send, grads = call(
        functools.partial(backward_kernel, labels, n, block),
        narrow + [shape_of((hidden, 2 * rows))],
        [scal, *gh_parts, c_gate, c_up, *wgu],
        [SMEM] + [VMEM] * (len(gh_parts) + 6),
        [pltpu.VMEM((rows, hidden), F32)],
        12 * rows * hidden * depth,
        8 * hidden * depth,
        8,
    )
    far = swap(grads)
    token_parts = to_owner(keep, send)

    (grad_down,) = call(
        down_kernel,
        [shape_of((hidden, depth))],
        [hid_turned, y_both],
        [VMEM] * 2,
        [pltpu.VMEM((hidden, depth), F32), pltpu.SemaphoreType.DMA((4,))],
        6 * rows * hidden * depth,
        4 * hidden * depth,
        10,
        HBM,
    )
    shapes = [(full, half_width)] * 2
    grad_gate, grad_up = call(
        weights_kernel,
        [shape_of(shape) for shape in shapes],
        [scal, grads, far, x_half],
        [SMEM] + [VMEM] * 3,
        [pltpu.VMEM(shape, F32) for shape in shapes] + [pltpu.SemaphoreType.DMA((16,))],
        12 * rows * half_width * full,
        8 * half_width * full,
        16,
        HBM,
    )
    output, grad_tokens = finish([output_parts, token_parts])
    return (
        output,
        grad_tokens,
        grad_gate.T.reshape(1, 1, half_width, full),
        grad_up.T.reshape(1, 1, half_width, full),
        grad_down.reshape(1, 1, hidden, depth),
    )


def solution(mesh):
    sizes = [mesh.shape[a] for a in ("rep", "width", "hid")]
    return jax.shard_map(
        functools.partial(shards, *sizes),
        mesh=mesh,
        in_specs=(
            P(("rep", "hid"), "width"),
            P(("rep", "hid"), "width"),
            P("width", "hid"),
            P("width", "hid"),
            P("hid", "width"),
        ),
        out_specs=(
            P(("rep", "hid"), "width"),
            P(("rep", "hid"), "width"),
            P("width", "rep", None, "hid"),
            P("width", "rep", None, "hid"),
            P("hid", "rep", None, "width"),
        ),
        check_vma=False,
    )
```
